32 devices in a mesh: area: 8 (over z, y), nrn: 4 (over x, core).
Axes of the slice: x: 2, y: 2, z: 4, core: 2. Of those that a mesh axis runs over, the one named last changes fastest.
Arguments:
- history: float32 [4, 4096, 128], P(None, ('area', 'nrn')), may hold values from -1 to 1
- drive: float32 [4096, 128], P(('area', 'nrn')), may hold values from -6 to 6
- leak: float32 [4096], P(('area', 'nrn')), may hold values from 0.1 to 0.9
- w_local: float32 [4096, 512], P(('area', 'nrn')), may hold values from -0.25 to 0.25
- w_long: float32 [4096, 4, 72], P(('area', 'nrn')), may hold values from -0.75 to 0.75
- sender_rows: int32 [32, 8, 9], P(('area', 'nrn')), may hold values from 0 to 127
- delays: int32 [8, 8], P('area'), may hold values from 1 to 4
- area_sizes: int32 [8], P('area'), may hold values from 256 to 512, as said below
Outputs:
- rates: float32 [4096, 128], P(('area', 'nrn'))
The draws below stay inside these ranges and needn't reach their ends.
Inputs may be any that keep to these rules, and one draw needn't show every extreme that they name: `area_sizes`: every area has at least half of its 512 slots live; some area has all of them live, some exactly half. `sender_rows`: indices may repeat.
All inputs are finite; a program needn't handle non-finite values.
Results may differ from the reference program's by a relative error of at most 0.0018.
Values may be sent and summed in bfloat16 or wider, within the bound.
No kernel may reach another device: no remote copies, remote signals or barrier semaphores. Data moves between devices by JAX's collectives and lax.ppermute only.
A program may use at most 64 MiB of HBM per device.

```python
import math
import jax
import jax.numpy as jnp
from jax import lax

BLK = 128
STIM = 128
PROJ_ROWS = 9
DMAX = 4
STEPS = 6
AREA_NEURONS = 512
BLOCKS = 32
NEURONS = 4096
N_AREA = 8
N_NRN = 4


def draw_area_sizes(key, part):
    first_key, second_key = jax.random.split(jax.random.fold_in(key, 11))
    sizes = jax.random.randint(first_key, (N_AREA,), AREA_NEURONS // 2, AREA_NEURONS + 1, dtype=jnp.int32)
    chosen = jax.random.randint(second_key, (), 0, N_AREA, dtype=jnp.int32)
    positions = jnp.arange(N_AREA, dtype=jnp.int32)
    sizes = jnp.where(positions == chosen, AREA_NEURONS, sizes)
    sizes = jnp.where(positions == (chosen + 1) % N_AREA, AREA_NEURONS // 2, sizes)
    return sizes.astype(jnp.int32)


def touch_ends(entries, key, smallest, high):
    longest = entries.shape.index(max(entries.shape))
    spots = []
    for shift in (0, 1):
        where = [jax.random.randint(jax.random.fold_in(key, axis), (), 0, length) for axis, length in enumerate(entries.shape)]
        where[longest] = (where[longest] + shift) % entries.shape[longest]
        spots.append(tuple(where))
    return entries.at[spots[0]].set(smallest).at[spots[1]].set(high)


def block_levels(rng, dims, cuts, low, high):
    loudness, own = 1.0, jax.random.fold_in(rng, 6)
    for position, blocks in cuts:
        heights = jnp.exp(jax.random.uniform(jax.random.fold_in(own, position), (blocks,), jnp.float32, low / len(cuts), high / len(cuts)))
        loudness = loudness * jnp.repeat(heights, dims[position] // blocks).reshape([-1 if axis == position else 1 for axis in range(len(dims))])
    return loudness


def gaussian(stream_key, dims, spread, reach, shards=(), held_as=jnp.bfloat16):
    entries = spread * jax.random.normal(stream_key, dims, jnp.float32)
    if shards:
        entries = entries * block_levels(stream_key, dims, shards, -0.22, 0.18)
    return jnp.clip(entries, -reach, reach).astype(held_as)


def setup_inputs(seed: int = 0) -> dict:
    key_list = jax.random.split(jax.random.key(seed), 9)
    return {
        "history": jnp.clip(jax.random.uniform(key_list[0], (DMAX, NEURONS, STIM), jnp.float32, -1.0, 1.0) * block_levels(key_list[0], (DMAX, NEURONS, STIM), ((1, 32),), -0.4, 0.0), -1.0, 1.0),
        "drive": gaussian(key_list[1], (NEURONS, STIM), 1.0, 6.0, ((0, 32),), jnp.float32),
        "leak": jnp.clip(jnp.exp(math.log(0.9) - 2.1972245 * jax.random.uniform(key_list[2], (NEURONS,), jnp.float32) ** block_levels(key_list[2], (NEURONS,), ((0, 32),), -0.2, 0.2)), 0.1, 0.9),
        "w_local": gaussian(key_list[3], (NEURONS, AREA_NEURONS), AREA_NEURONS ** -0.5, 0.25, ((0, 32),), jnp.float32),
        "w_long": gaussian(key_list[4], (NEURONS, N_NRN, N_AREA * PROJ_ROWS), (N_AREA * PROJ_ROWS) ** -0.5, 0.75, ((0, 32),), jnp.float32),
        "sender_rows": touch_ends(jax.random.randint(key_list[5], (BLOCKS, N_AREA, PROJ_ROWS), 0, BLK), jax.random.fold_in(key_list[5], 1), 0, BLK - 1).astype(jnp.int32),
        "delays": touch_ends(jax.random.randint(key_list[6], (N_AREA, N_AREA), 1, DMAX + 1), jax.random.fold_in(key_list[6], 1), 1, DMAX).astype(jnp.int32),
        "area_sizes": draw_area_sizes(jax.random.fold_in(key_list[8], 71), 0),
    }


def unround(values):
    return lax.optimization_barrier(values).astype(jnp.float32)


def reference(history, drive, leak, w_local, w_long, sender_rows, delays, area_sizes):
    area_width = N_NRN * BLK
    neurons = history.shape[1]
    blocks = N_AREA * N_NRN
    positions = jnp.arange(neurons, dtype=jnp.int32)
    active = ((positions % area_width) < area_sizes[positions // area_width]).astype(jnp.float32)[:, None]
    states = history * active[None]
    block_ids = jnp.arange(blocks, dtype=jnp.int32)
    for iteration in range(STEPS):
        block_view = states.reshape(DMAX, blocks, BLK, STIM)
        current = unround(states[0].astype(jnp.bfloat16))

        def area_input(area_id):
            lagged = jnp.repeat(delays[:, area_id] - 1, N_NRN)
            chosen = sender_rows[:, area_id, :]
            gathered = block_view[lagged[:, None], block_ids[:, None], chosen]
            gathered = unround(gathered.astype(jnp.bfloat16))
            gathered = gathered.reshape(N_AREA, N_NRN, PROJ_ROWS, STIM).transpose(1, 0, 2, 3).reshape(-1, STIM)
            start = (area_id * area_width).astype(jnp.int32)
            weights = lax.dynamic_slice_in_dim(w_long, start, area_width, 0).reshape(area_width, -1)
            long_term = jnp.dot(weights, gathered, precision=lax.Precision.HIGHEST, preferred_element_type=jnp.float32)
            local_rows = lax.dynamic_slice_in_dim(current, start, area_width, 0)
            local_weights = lax.dynamic_slice_in_dim(w_local, start, area_width, 0)
            return long_term + jnp.dot(local_weights, local_rows, precision=lax.Precision.HIGHEST, preferred_element_type=jnp.float32)

        inputs = lax.map(area_input, jnp.arange(N_AREA, dtype=jnp.int32)).reshape(neurons, STIM) + drive
        updated = active * (states[0] + leak[:, None] * (jnp.tanh(inputs) - states[0]))
        states = jnp.concatenate([updated[None], states[:-1]], axis=0)
    return states[0]
```

```python
import functools
import math

import jax
import jax.numpy as jnp
from jax import lax
from jax.experimental import pallas as pl
from jax.experimental.pallas import tpu as pltpu
from jax.sharding import PartitionSpec as P

STEPS = 6
SLOT = 16
SCALE = 2.0**15
F32, BF16 = jnp.float32, jnp.bfloat16
VMEM = pl.BlockSpec(memory_space=pltpu.VMEM)
SMEM = pl.BlockSpec(memory_space=pltpu.SMEM)


def split(values):
    high = lax.reduce_precision(values, 8, 7)
    return high.astype(BF16), (values - high).astype(BF16)


def rows_of(index, count):
    return pl.ds(pl.multiple_of(index * count, count), count)


def choices(meta, columns, width):
    picks = []
    lanes = lax.broadcasted_iota(jnp.int32, (meta.shape[0], width), 1).astype(F32)
    for column in range(columns):
        row = meta[:, 2 + column : 3 + column].astype(F32)
        lag = meta[:, 2 + columns + column : 3 + columns + column].astype(F32)
        picks.append((lanes == row + lag * meta.shape[0]).astype(F32).astype(BF16))
    return jnp.concatenate(picks, axis=0)


def first_kernel(group, columns, misc_ref, out_ref):
    block = misc_ref.shape[0]
    depth = 4
    past = jnp.concatenate([misc_ref[:, i * block : (i + 1) * block] for i in range(depth)], axis=0)
    chosen = choices(misc_ref[:, (depth + 3) * block :], columns, depth * block)
    picked = jnp.dot(chosen, past, preferred_element_type=F32).astype(BF16)
    areas = out_ref.shape[0] // group
    for area in range(areas):
        for member in range(group):
            out_ref[area * group + member] = picked[area * SLOT : (area + 1) * SLOT]


def prepare_kernel(group, columns, me_ref, *refs):
    misc = refs[:group]
    state_ref, drive_ref, rate_ref, choice_ref = refs[group : group + 4]
    past = refs[group + 4 :]
    block = misc[0].shape[0]
    for slot in range(group):
        piece = misc[slot]
        owner = rows_of(me_ref[0] ^ slot, block)
        for age, ref in enumerate(past):
            ref[owner, :] = piece[:, age * block : (age + 1) * block]
        take = lambda i: piece[:, i * block : (i + 1) * block].astype(F32)
        state_ref[slot] = take(0) + take(len(past))
        drive_ref[slot] = take(len(past) + 1) + take(len(past) + 2)
        meta = piece[:, (len(past) + 3) * block :]
        rate = meta[:, 0:1].astype(F32) + meta[:, 1:2].astype(F32)
        rate_ref[slot] = jnp.broadcast_to(rate, rate_ref.shape[1:])
        choice_ref[slot] = choices(meta, columns, len(past) * block)


def step_kernel(group, last, me_ref, *refs):
    high, low = refs[:group], refs[group : 2 * group]
    received, state_ref, drive_ref, rate_ref, choice_ref = refs[2 * group : 2 * group + 5]
    past = refs[2 * group + 5 : 2 * group + 9]
    outs = refs[2 * group + 9 :]
    block, stimuli = state_ref.shape[1:]
    local = group * block
    for slot in range(1 if last else group):
        total = jnp.dot(high[slot][:, :local], past[0][...], preferred_element_type=F32)
        total += jnp.dot(low[slot][:, :local], past[0][...], preferred_element_type=F32)
        total += jnp.dot(high[slot][:, local:], received[...], preferred_element_type=F32)
        total += jnp.dot(low[slot][:, local:], received[...], preferred_element_type=F32)
        inputs = total * (1.0 / SCALE) + drive_ref[slot]
        state = state_ref[slot]
        new = state + rate_ref[slot] * (jnp.tanh(inputs) - state)
        if last:
            outs[0][...] = new
            continue
        new_state_ref, new_past_ref, out_ref = outs
        owner = me_ref[0] ^ slot
        rounded = new.astype(BF16)
        new_state_ref[slot] = new
        new_past_ref[rows_of(owner, block), :] = rounded
        older = [past[age][rows_of(owner, block), :] for age in range(len(past) - 1)]
        recent = jnp.concatenate([rounded] + older, axis=0)
        picked = jnp.dot(choice_ref[slot], recent, preferred_element_type=F32).astype(BF16)
        for area in range(out_ref.shape[0]):
            out_ref[area, rows_of(owner, SLOT), :] = picked[area * SLOT : (area + 1) * SLOT]


def call(kernel, out_shape, operands, index=None):
    shapes = out_shape if isinstance(out_shape, list) else [out_shape]
    held = sum(math.prod(v.shape) * v.dtype.itemsize for v in [*shapes, *operands])
    scalars = [] if index is None else [index]
    return pl.pallas_call(
        kernel,
        out_shape=out_shape,
        in_specs=[SMEM] * len(scalars) + [VMEM] * len(operands),
        out_specs=[VMEM] * len(shapes) if isinstance(out_shape, list) else VMEM,
        compiler_params=pltpu.CompilerParams(vmem_limit_bytes=held + (4 << 20)),
    )(*scalars, *operands)


def local(group, history, drive, leak, w_local, w_long, sender_rows, delays, area_sizes):
    depth, block, stimuli = history.shape
    areas, senders = sender_rows.shape[1:]
    me = lax.axis_index("nrn")
    offsets = me * block + jnp.arange(block, dtype=jnp.int32)
    active = (offsets < area_sizes[0]).astype(F32)
    states = history * active[None, :, None]

    long = w_long.reshape(block, group, areas, senders).transpose(0, 2, 1, 3)
    long = jnp.pad(long, ((0, 0), (0, 0), (0, 0), (0, SLOT - senders))).reshape(block, -1)
    weights = jnp.concatenate([w_local, long], axis=1) * SCALE
    shipped = weights.astype(jnp.float16)

    columns = areas * SLOT // block
    spread = lambda table, fill: jnp.pad(
        table, ((0, 0), (0, SLOT - senders)), constant_values=fill
    ).reshape(columns, block).T.astype(BF16)
    rate_high, rate_low = split(active * leak)
    meta = jnp.concatenate(
        [
            rate_high[:, None],
            rate_low[:, None],
            spread(sender_rows[0], 0),
            spread(jnp.broadcast_to(delays[0][:, None] - 1, (areas, senders)), depth),
        ],
        axis=1,
    )
    meta = jnp.pad(meta, ((0, 0), (0, -meta.shape[1] % 128)))
    now_high, now_low = split(states[0])
    drive_high, drive_low = split(drive)
    misc = jnp.concatenate(
        [now_high]
        + [states[i].astype(BF16) for i in range(1, depth)]
        + [now_low, drive_high, drive_low, meta],
        axis=1,
    )

    swap = lambda values, bit: lax.ppermute(
        values, "nrn", [(i, i ^ bit) for i in range(group)]
    )
    ship = [(shipped, misc)]
    bit = group // 2
    ship += [jax.tree.map(lambda v: swap(v, bit), ship[0])]
    first = call(
        functools.partial(first_kernel, group, columns),
        jax.ShapeDtypeStruct((areas * group, SLOT, stimuli), BF16),
        [misc],
    )
    received = lax.all_to_all(first, ("area", "nrn"), split_axis=0, concat_axis=0, tiled=True)
    pieces = {0: ship[0], bit: ship[1]}
    while bit > 1:
        bit //= 2
        for slot in list(pieces):
            pieces[slot ^ bit] = jax.tree.map(lambda v: swap(v, bit), pieces[slot])
    highs, lows = [], []
    for slot in range(group):
        whole = weights if slot == 0 else pieces[slot][0].astype(F32)
        high, low = split(whole)
        highs.append(high)
        lows.append(low)
    miscs = [pieces[slot][1] for slot in range(group)]
    index = me.astype(jnp.int32).reshape(1)
    cube = jax.ShapeDtypeStruct((group, block, stimuli), F32)
    flat = jax.ShapeDtypeStruct((group * block, stimuli), BF16)
    prepared = call(
        functools.partial(prepare_kernel, group, columns),
        [cube, cube, cube, jax.ShapeDtypeStruct((group, areas * SLOT, depth * block), BF16)]
        + [flat] * depth,
        miscs,
        index,
    )
    state, drives, rates, chosen = prepared[:4]
    past = list(prepared[4:])
    for iteration in range(STEPS):
        final = iteration == STEPS - 1
        if final:
            shapes = jax.ShapeDtypeStruct((block, stimuli), F32)
        else:
            shapes = [cube, flat, jax.ShapeDtypeStruct((areas, group * SLOT, stimuli), BF16)]
        result = call(
            functools.partial(step_kernel, group, final),
            shapes,
            [*highs, *lows, received.reshape(-1, stimuli), state, drives, rates, chosen, *past],
            index,
        )
        if final:
            return result
        state, newest, outgoing = result
        past = [newest] + past[:-1]
        received = lax.all_to_all(outgoing, "area", split_axis=0, concat_axis=0, tiled=True)


def solution(mesh):
    placed = (
        P(None, ("area", "nrn"), None),
        P(("area", "nrn"), None),
        P(("area", "nrn")),
        P(("area", "nrn"), None),
        P(("area", "nrn"), None, None),
        P(("area", "nrn"), None, None),
        P("area", None),
        P("area"),
    )
    return jax.shard_map(
        functools.partial(local, mesh.shape["nrn"]),
        mesh=mesh,
        in_specs=placed,
        out_specs=P(("area", "nrn"), None),
        check_vma=False,
    )
```

```python
import functools
import math

import jax
import jax.numpy as jnp
from jax import lax
from jax.experimental import pallas as pl
from jax.experimental.pallas import tpu as pltpu
from jax.sharding import PartitionSpec as P

STEPS = 6
SLOT = 16
TERMS = 3
F32, BF16 = jnp.float32, jnp.bfloat16
VMEM = pl.BlockSpec(memory_space=pltpu.VMEM)


def iota(shape, axis):
    return lax.broadcasted_iota(jnp.int32, shape, axis)


def terms_of(values):
    terms = []
    for _ in range(TERMS):
        terms.append(values.astype(BF16))
        values = values - terms[-1].astype(F32)
    return terms


def column(line):
    width = line.shape[1]
    eye = iota((width, width), 0) == iota((width, width), 1)
    return jnp.sum(jnp.where(eye, jnp.broadcast_to(line, eye.shape), 0.0), axis=1, keepdims=True)


def send(picked, out_ref, group):
    for area in range(out_ref.shape[0] // group):
        for member in range(group):
            out_ref[area * group + member] = picked[area * SLOT : (area + 1) * SLOT]


def pack_kernel(group, senders, *refs):
    given, outs, scratch = refs[:7], refs[7:-9], refs[-9:]
    held, padded, sems = scratch[:7], scratch[7], scratch[8]
    weights, state, rate, choice, outgoing, *past = outs
    copies = [
        pltpu.make_async_copy(src, dst, sems.at[i]) for i, (src, dst) in enumerate(zip(given, held))
    ]
    for copy in copies:
        copy.start()
    for copy in copies:
        copy.wait()
    history, leak, w_local, w_long, table, lags, sizes = held
    depth, block = history.shape[:2]
    areas = table.shape[0]
    me = lax.axis_index("nrn")
    active = (iota((block, 1), 0) + me * block < sizes[0:1, 0:1]).astype(F32)
    state[...] = history[0] * active
    for age in range(depth):
        past[age][...] = (history[age] * active).astype(BF16)
    rate[...] = jnp.broadcast_to(active * column(leak[...]), rate.shape)

    lines = jnp.concatenate(
        [table[...].astype(F32), jnp.zeros((areas, SLOT - senders), F32)], axis=1
    )
    real = iota((SLOT, 1), 0) < senders
    places = []
    for area in range(areas):
        age = lags[0:1, area : area + 1].astype(F32) - 1.0
        age = jnp.where(real, jnp.broadcast_to(age, real.shape), float(depth))
        places.append(column(lines[area : area + 1]) + age * block)
    lanes = iota((areas * SLOT, depth * block), 1).astype(F32)
    choice[...] = (lanes == jnp.concatenate(places, axis=0)).astype(F32).astype(BF16)
    recent = jnp.concatenate([ref[...] for ref in past], axis=0)
    send(jnp.dot(choice[...], recent, preferred_element_type=F32).astype(BF16), outgoing, group)

    near = w_local.shape[1]
    for term, values in enumerate(terms_of(w_local[...])):
        weights[term * block : (term + 1) * block, :near] = values
    blank = jnp.zeros((SLOT - senders, block), F32)
    for area in range(areas):
        for member in range(group):
            spot = (area * group + member) * SLOT
            piece = w_long[member, area * senders : (area + 1) * senders, :]
            padded[spot : spot + SLOT, :] = jnp.concatenate([piece, blank], axis=0)
    for part in range(padded.shape[0] // block):
        tile = padded[part * block : (part + 1) * block, :].T
        for term, values in enumerate(terms_of(tile)):
            spot = near + part * block
            weights[term * block : (term + 1) * block, spot : spot + block] = values


def step_kernel(group, depth, last, *refs):
    (weights, received, state, drive, rate, choice), refs = refs[:6], refs[6:]
    mates, past, refs = refs[:group], refs[group : group + depth - 1], refs[group + depth - 1 :]
    current, outs = refs[-1], refs[:-1]
    block = state.shape[0]
    near = group * block
    me = lax.axis_index("nrn")
    for slot in range(group):
        start = pl.multiple_of((me ^ slot) * block, block)
        current[pl.ds(start, block), :] = mates[slot][...]
    total = jnp.dot(weights[:, :near], current[...], preferred_element_type=F32)
    total += jnp.dot(weights[:, near:], received[...], preferred_element_type=F32)
    parts = [total[term * block : (term + 1) * block] for term in range(TERMS)]
    inputs = functools.reduce(lambda a, b: a + b, reversed(parts)) + drive[...]
    old = state[...]
    new = old + rate[...] * (jnp.tanh(inputs) - old)
    if last:
        outs[0][...] = new
        return
    new_state, newest, outgoing = outs
    new_state[...] = new
    newest[...] = new.astype(BF16)
    recent = jnp.concatenate([new.astype(BF16), mates[0][...]] + [ref[...] for ref in past[:-1]], axis=0)
    send(jnp.dot(choice[...], recent, preferred_element_type=F32).astype(BF16), outgoing, group)


def call(kernel, out_shape, operands, scratch=(), **settings):
    size = lambda value: math.prod(value.shape) * value.dtype.itemsize
    held = sum(map(size, [*out_shape, *operands]))
    return pl.pallas_call(
        kernel,
        out_shape=out_shape,
        out_specs=[VMEM] * len(out_shape),
        compiler_params=pltpu.CompilerParams(vmem_limit_bytes=held + (4 << 20)),
        scratch_shapes=scratch,
        **{"in_specs": [VMEM] * len(operands), **settings},
    )(*operands)


def local(group, history, drive, leak, w_local, w_long, sender_rows, delays, area_sizes):
    depth, block, stimuli = history.shape
    areas, senders = sender_rows.shape[1:]
    near, far = group * block, areas * group * SLOT
    shape = jax.ShapeDtypeStruct
    tile = lambda kind: shape((block, stimuli), kind)
    sent = shape((areas * group, SLOT, stimuli), BF16)
    given = [
        history,
        leak.reshape(1, block),
        w_local,
        w_long.transpose(1, 2, 0),
        sender_rows[0],
        delays,
        area_sizes.reshape(1, 1),
    ]
    stay = lambda v: pltpu.with_memory_space_constraint(v, pltpu.HBM) if v.size > 1 else v
    weights, state, rate, choice, outgoing, *past = call(
        functools.partial(pack_kernel, group, senders),
        [
            shape((TERMS * block, near + far), BF16),
            tile(F32),
            tile(F32),
            shape((areas * SLOT, depth * block), BF16),
            sent,
            *[tile(BF16)] * depth,
        ],
        [stay(v) for v in given],
        [pltpu.VMEM(v.shape, v.dtype) for v in given]
        + [pltpu.VMEM((far, block), F32), pltpu.SemaphoreType.DMA((len(given),))],
        in_specs=[pl.BlockSpec(memory_space=pl.ANY)] * len(given),
    )
    swap = lambda v, bits: lax.ppermute(v, "nrn", [(i, i ^ bits) for i in range(group)])
    for iteration in range(STEPS):
        final = iteration == STEPS - 1
        mates = [swap(past[0], bits) for bits in range(1, group)]
        received = lax.all_to_all(outgoing, ("area", "nrn"), split_axis=0, concat_axis=0, tiled=True)
        received, mates = lax.optimization_barrier((received, mates))
        result = call(
            functools.partial(step_kernel, group, depth, final),
            [tile(F32)] if final else [tile(F32), tile(BF16), sent],
            [weights, received.reshape(far, stimuli), state, drive, rate, choice, past[0], *mates, *past[1:]],
            [pltpu.VMEM((near, stimuli), BF16)],
        )
        if final:
            return result[0]
        state, newest, outgoing = result
        past = [newest, *past[:-1]]


def solution(mesh):
    placed = (
        P(None, ("area", "nrn"), None),
        P(("area", "nrn"), None),
        P(("area", "nrn")),
        P(("area", "nrn"), None),
        P(("area", "nrn"), None, None),
        P(("area", "nrn"), None, None),
        P("area", None),
        P("area"),
    )
    return jax.shard_map(
        functools.partial(local, mesh.shape["nrn"]),
        mesh=mesh,
        in_specs=placed,
        out_specs=P(("area", "nrn"), None),
        check_vma=False,
    )
```

```python
import functools
import math

import jax
import jax.numpy as jnp
from jax import lax
from jax.experimental import pallas as pl
from jax.experimental.pallas import tpu as pltpu
from jax.sharding import PartitionSpec as P

STEPS = 6
PAIR = 2
TERMS = 3
F32, BF16 = jnp.float32, jnp.bfloat16
VMEM = pl.BlockSpec(memory_space=pltpu.VMEM)


def iota(shape, axis):
    return lax.broadcasted_iota(jnp.int32, shape, axis)


def terms_of(values):
    terms = []
    for _ in range(TERMS):
        terms.append(values.astype(BF16))
        values = values - terms[-1].astype(F32)
    return terms


def column(line):
    width = line.shape[1]
    eye = iota((width, width), 0) == iota((width, width), 1)
    return jnp.sum(jnp.where(eye, jnp.broadcast_to(line, eye.shape), 0.0), axis=1, keepdims=True)


def send(picked, out_ref, group):
    stimuli = picked.shape[1]
    areas = out_ref.shape[0] // group
    for tile in range(out_ref.shape[2] // stimuli):
        for area in range(areas):
            start = (tile * areas + area) * PAIR
            for member in range(group):
                spot = (area * group + member, slice(None), slice(tile * stimuli, (tile + 1) * stimuli))
                out_ref[spot] = picked[start : start + PAIR]


def rows_from(chunks, stimuli):
    tiles = [chunks[:, :, start : start + stimuli] for start in range(0, chunks.shape[2], stimuli)]
    return jnp.concatenate([tile.reshape(-1, stimuli) for tile in tiles], axis=0)


def pack_kernel(group, senders, *refs):
    given, outs, scratch = refs[:7], refs[7:-9], refs[-9:]
    held, padded, sems = scratch[:7], scratch[7], scratch[8]
    weights, state, rate, choice, outgoing, *past = outs
    copies = [
        pltpu.make_async_copy(src, dst, sems.at[i]) for i, (src, dst) in enumerate(zip(given, held))
    ]
    for copy in copies:
        copy.start()
    for copy in copies:
        copy.wait()
    history, leak, w_local, w_long, table, lags, sizes = held
    depth, block = history.shape[:2]
    areas = table.shape[0]
    me = lax.axis_index("nrn")
    active = (iota((block, 1), 0) + me * block < sizes[0:1, 0:1]).astype(F32)
    state[...] = history[0] * active
    for age in range(depth):
        past[age][...] = (history[age] * active).astype(BF16)
    rate[...] = jnp.broadcast_to(active * column(leak[...]), rate.shape)

    tiles = -(-senders // PAIR)
    wide = (areas * PAIR, areas)
    mine = iota(wide, 1) == iota(wide, 0) // PAIR
    spread = jnp.dot(
        mine.astype(F32).astype(BF16), table[...].astype(F32).astype(BF16), preferred_element_type=F32
    )
    delay = jnp.broadcast_to(lags[...].astype(F32) - 1.0, wide)
    age = jnp.sum(jnp.where(mine, delay, 0.0), axis=1, keepdims=True)
    half = iota((areas * PAIR, 1), 0) % PAIR
    places = []
    for tile in range(tiles):
        sender = half * tiles + tile
        row = jnp.sum(jnp.where(iota(spread.shape, 1) == sender, spread, 0.0), axis=1, keepdims=True)
        places.append(row + jnp.where(sender < senders, age, float(depth)) * block)
    lanes = iota(choice.shape, 1).astype(F32)
    choice[...] = (lanes == jnp.concatenate(places, axis=0)).astype(F32).astype(BF16)
    recent = jnp.concatenate([ref[...] for ref in past], axis=0)
    send(jnp.dot(choice[...], recent, preferred_element_type=F32).astype(BF16), outgoing, group)

    near = w_local.shape[1]
    for term, values in enumerate(terms_of(w_local[...])):
        weights[term * block : (term + 1) * block, :near] = values
    chunks = areas * group
    far = tiles * chunks * PAIR
    last = (tiles - 1) * chunks * PAIR
    padded[last:, :] = jnp.zeros((padded.shape[0] - last, block), F32)
    for area in range(areas):
        for member in range(group):
            for side in range(PAIR):
                first = side * tiles
                count = min(tiles, senders - first)
                rows = pl.ds((area * group + member) * PAIR + side, count, stride=chunks * PAIR)
                padded[rows, :] = w_long[member, pl.ds(area * senders + first, count), :]
    for part in range(padded.shape[0] // block):
        tile = padded[part * block : (part + 1) * block, :].T
        width = min(block, far - part * block)
        for term, values in enumerate(terms_of(tile)):
            spot = near + part * block
            weights[term * block : (term + 1) * block, spot : spot + width] = values[:, :width]


def step_kernel(group, depth, last, *refs):
    (weights, received, state, drive, rate, choice), refs = refs[:6], refs[6:]
    mates, past, refs = refs[:group], refs[group : group + depth - 1], refs[group + depth - 1 :]
    current, outs = refs[-1], refs[:-1]
    block = state.shape[0]
    near = group * block
    me = lax.axis_index("nrn")
    for slot in range(group):
        start = pl.multiple_of((me ^ slot) * block, block)
        current[pl.ds(start, block), :] = mates[slot][...]
    total = jnp.dot(weights[:, :near], current[...], preferred_element_type=F32)
    sent = rows_from(received[...], state.shape[1])
    total += jnp.dot(weights[:, near:], sent, preferred_element_type=F32)
    parts = [total[term * block : (term + 1) * block] for term in range(TERMS)]
    inputs = functools.reduce(lambda a, b: a + b, reversed(parts)) + drive[...]
    old = state[...]
    new = old + rate[...] * (jnp.tanh(inputs) - old)
    if last:
        outs[0][...] = new
        return
    new_state, newest, outgoing = outs
    new_state[...] = new
    newest[...] = new.astype(BF16)
    recent = jnp.concatenate([new.astype(BF16), mates[0][...]] + [ref[...] for ref in past[:-1]], axis=0)
    send(jnp.dot(choice[...], recent, preferred_element_type=F32).astype(BF16), outgoing, group)


def call(kernel, out_shape, operands, scratch=(), **settings):
    size = lambda value: math.prod(value.shape) * value.dtype.itemsize
    held = sum(map(size, [*out_shape, *operands]))
    return pl.pallas_call(
        kernel,
        out_shape=out_shape,
        out_specs=[VMEM] * len(out_shape),
        compiler_params=pltpu.CompilerParams(vmem_limit_bytes=held + (4 << 20)),
        scratch_shapes=scratch,
        **{"in_specs": [VMEM] * len(operands), **settings},
    )(*operands)


def local(group, history, drive, leak, w_local, w_long, sender_rows, delays, area_sizes):
    depth, block, stimuli = history.shape
    areas, senders = sender_rows.shape[1:]
    tiles = -(-senders // PAIR)
    near, far = group * block, areas * group * tiles * PAIR
    shape = jax.ShapeDtypeStruct
    tile = lambda kind: shape((block, stimuli), kind)
    sent = shape((areas * group, PAIR, tiles * stimuli), BF16)
    given = [
        history,
        leak.reshape(1, block),
        w_local,
        w_long.transpose(1, 2, 0),
        sender_rows[0],
        delays,
        area_sizes.reshape(1, 1),
    ]
    stay = lambda v: pltpu.with_memory_space_constraint(v, pltpu.HBM) if v.size > 1 else v
    weights, state, rate, choice, outgoing, *past = call(
        functools.partial(pack_kernel, group, senders),
        [
            shape((TERMS * block, near + far), BF16),
            tile(F32),
            tile(F32),
            shape((areas * tiles * PAIR, depth * block), BF16),
            sent,
            *[tile(BF16)] * depth,
        ],
        [stay(v) for v in given],
        [pltpu.VMEM(v.shape, v.dtype) for v in given]
        + [pltpu.VMEM((far + -far % block, block), F32), pltpu.SemaphoreType.DMA((len(given),))],
        in_specs=[pl.BlockSpec(memory_space=pl.ANY)] * len(given),
    )
    swap = lambda v, bits: lax.ppermute(v, "nrn", [(i, i ^ bits) for i in range(group)])
    for iteration in range(STEPS):
        final = iteration == STEPS - 1
        mates = [swap(past[0], bits) for bits in range(1, group)]
        received = lax.all_to_all(outgoing, ("area", "nrn"), split_axis=0, concat_axis=0, tiled=True)
        received, mates = lax.optimization_barrier((received, mates))
        result = call(
            functools.partial(step_kernel, group, depth, final),
            [tile(F32)] if final else [tile(F32), tile(BF16), sent],
            [weights, received, state, drive, rate, choice, past[0], *mates, *past[1:]],
            [pltpu.VMEM((near, stimuli), BF16)],
        )
        if final:
            return result[0]
        state, newest, outgoing = result
        past = [newest, *past[:-1]]


def solution(mesh):
    placed = (
        P(None, ("area", "nrn"), None),
        P(("area", "nrn"), None),
        P(("area", "nrn")),
        P(("area", "nrn"), None),
        P(("area", "nrn"), None, None),
        P(("area", "nrn"), None, None),
        P("area", None),
        P("area"),
    )
    return jax.shard_map(
        functools.partial(local, mesh.shape["nrn"]),
        mesh=mesh,
        in_specs=placed,
        out_specs=P(("area", "nrn"), None),
        check_vma=False,
    )
```

```python
import functools
import math

import jax
import jax.numpy as jnp
from jax import lax
from jax.experimental import pallas as pl
from jax.experimental.pallas import tpu as pltpu
from jax.sharding import PartitionSpec as P

STEPS = 6
PAIR = 2
TERMS = 3
F32, BF16 = jnp.float32, jnp.bfloat16
VMEM = pl.BlockSpec(memory_space=pltpu.VMEM)
HBM = pl.BlockSpec(memory_space=pl.ANY)


def iota(shape, axis):
    return lax.broadcasted_iota(jnp.int32, shape, axis)


def terms_of(values):
    terms = []
    for _ in range(TERMS):
        terms.append(values.astype(BF16))
        values = values - terms[-1].astype(F32)
    return terms


def column(line):
    width = line.shape[1]
    eye = iota((width, width), 0) == iota((width, width), 1)
    return jnp.sum(jnp.where(eye, jnp.broadcast_to(line, eye.shape), 0.0), axis=1, keepdims=True)


def send(picked, chunks, out_ref, sems):
    stimuli = picked.shape[1]
    areas = chunks.shape[0]
    for tile in range(chunks.shape[2] // stimuli):
        for area in range(areas):
            start = (tile * areas + area) * PAIR
            chunks[area, :, tile * stimuli : (tile + 1) * stimuli] = picked[start : start + PAIR]
    copies = [
        pltpu.make_async_copy(chunks, out_ref.at[:, member], sems.at[member])
        for member in range(out_ref.shape[1])
    ]
    for copy in copies:
        copy.start()
    return copies


def rows_from(chunks, stimuli):
    tiles = [chunks[:, :, start : start + stimuli] for start in range(0, chunks.shape[2], stimuli)]
    return jnp.concatenate([tile.reshape(-1, stimuli) for tile in tiles], axis=0)


def pack_kernel(group, senders, *refs):
    given, outs, scratch = refs[:7], refs[7:-11], refs[-11:]
    held, (padded, chunks_ref, sems, send_sems) = scratch[:7], scratch[7:]
    outgoing, weights, state, rate, choice, older, *past = outs
    copies = [
        pltpu.make_async_copy(src, dst, sems.at[i]) for i, (src, dst) in enumerate(zip(given, held))
    ]
    for copy in copies:
        copy.start()
    for i in (4, 5, 6, 1, 0):
        copies[i].wait()
    history, leak, w_local, w_long, table, lags, sizes = held
    depth, block = history.shape[:2]
    areas = table.shape[0]
    me = lax.axis_index("nrn")
    active = (iota((block, 1), 0) + me * block < sizes[0]).astype(F32)
    state[...] = history[0] * active
    rate[...] = jnp.broadcast_to(active * column(leak[...]), rate.shape)

    tiles = -(-senders // PAIR)
    wide = (areas * PAIR, areas)
    mine = iota(wide, 1) == iota(wide, 0) // PAIR
    spread = jnp.dot(
        mine.astype(F32).astype(BF16), table[...].astype(F32).astype(BF16), preferred_element_type=F32
    )
    delay = jnp.broadcast_to(lags[...].astype(F32) - 1.0, wide)
    age = jnp.sum(jnp.where(mine, delay, 0.0), axis=1, keepdims=True)
    half = iota((areas * PAIR, 1), 0) % PAIR
    places = []
    for tile in range(tiles):
        sender = half * tiles + tile
        row = jnp.sum(jnp.where(iota(spread.shape, 1) == sender, spread, 0.0), axis=1, keepdims=True)
        places.append(row + jnp.where(sender < senders, age, float(depth)) * block)
    lanes = iota(choice.shape, 1).astype(F32)
    choice[...] = (lanes == jnp.concatenate(places, axis=0)).astype(F32).astype(BF16)
    rows = [(history[age] * active).astype(BF16) for age in range(depth)]
    picked = jnp.dot(choice[...], jnp.concatenate(rows, axis=0), preferred_element_type=F32)
    sent = send(picked.astype(BF16), chunks_ref, outgoing, send_sems)
    older[...] = jnp.dot(
        choice[:, block:], jnp.concatenate(rows[:-1], axis=0), preferred_element_type=F32
    )
    for ref, values in zip(past, rows):
        ref[...] = values

    for i in (2, 3):
        copies[i].wait()
    near = w_local.shape[1]
    for term, values in enumerate(terms_of(w_local[...])):
        weights[term * block : (term + 1) * block, :near] = values
    chunks = areas * group
    far = tiles * chunks * PAIR
    last = (tiles - 1) * chunks * PAIR
    padded[last:, :] = jnp.zeros((padded.shape[0] - last, block), F32)
    for area in range(areas):
        for member in range(group):
            for side in range(PAIR):
                first = side * tiles
                count = min(tiles, senders - first)
                rows = pl.ds((area * group + member) * PAIR + side, count, stride=chunks * PAIR)
                padded[rows, :] = w_long[member, pl.ds(area * senders + first, count), :]
    for part in range(padded.shape[0] // block):
        tile = padded[part * block : (part + 1) * block, :].T
        width = min(block, far - part * block)
        for term, values in enumerate(terms_of(tile)):
            spot = near + part * block
            weights[term * block : (term + 1) * block, spot : spot + width] = values[:, :width]
    for copy in sent:
        copy.wait()


def step_kernel(group, left, *refs):
    (weights, received, state, drive, rate), mates = refs[:5], refs[5 : 5 + group]
    refs = refs[5 + group :]
    outs, current = refs[:-3] if left else refs[:-1], refs[-1]
    block = state.shape[0]
    near = group * block
    me = lax.axis_index("nrn")
    for slot in range(group):
        start = pl.multiple_of((me ^ slot) * block, block)
        current[pl.ds(start, block), :] = mates[slot][...]
    total = jnp.dot(weights[:, :near], current[...], preferred_element_type=F32)
    sent = rows_from(received[...], state.shape[1])
    total += jnp.dot(weights[:, near:], sent, preferred_element_type=F32)
    parts = [total[term * block : (term + 1) * block] for term in range(TERMS)]
    inputs = functools.reduce(lambda a, b: a + b, reversed(parts)) + drive[...]
    old = state[...]
    new = old + rate[...] * (jnp.tanh(inputs) - old)
    if not left:
        outs[0][...] = new
        return
    (choice, older, *past), (outgoing, new_state, newest, *next_older) = outs[:left], outs[left:]
    rounded = new.astype(BF16)
    picked = older[...] + jnp.dot(choice[:, :block], rounded, preferred_element_type=F32)
    copies = send(picked.astype(BF16), refs[-3], outgoing, refs[-2])
    new_state[...] = new
    newest[...] = rounded
    rows = jnp.concatenate([rounded, mates[0][...]] + [ref[...] for ref in past], axis=0)
    for ref in next_older:
        ref[...] = jnp.dot(choice[:, block:], rows, preferred_element_type=F32)
    for copy in copies:
        copy.wait()


def call(kernel, out_shape, operands, scratch=(), **settings):
    size = lambda value: math.prod(value.shape) * value.dtype.itemsize
    held = sum(map(size, [*out_shape, *operands]))
    return pl.pallas_call(
        kernel,
        out_shape=out_shape,
        out_specs=[HBM if len(value.shape) == 4 else VMEM for value in out_shape],
        compiler_params=pltpu.CompilerParams(vmem_limit_bytes=held + (4 << 20)),
        scratch_shapes=scratch,
        **{"in_specs": [VMEM] * len(operands), **settings},
    )(*operands)


def local(group, history, drive, leak, w_local, w_long, sender_rows, delays, area_sizes):
    depth, block, stimuli = history.shape
    areas, senders = sender_rows.shape[1:]
    tiles = -(-senders // PAIR)
    near, far = group * block, areas * group * tiles * PAIR
    shape = jax.ShapeDtypeStruct
    tile = lambda kind: shape((block, stimuli), kind)
    sent = shape((areas, group, PAIR, tiles * stimuli), BF16)
    elder = shape((areas * tiles * PAIR, stimuli), F32)
    sending = [pltpu.VMEM((areas, PAIR, tiles * stimuli), BF16), pltpu.SemaphoreType.DMA((group,))]
    given = [
        history,
        leak.reshape(1, block),
        w_local,
        w_long.transpose(1, 2, 0),
        sender_rows[0],
        delays,
        area_sizes,
    ]
    stay = lambda v: pltpu.with_memory_space_constraint(v, pltpu.HBM) if v.size > 1 else v
    outgoing, weights, state, rate, choice, *rest = call(
        functools.partial(pack_kernel, group, senders),
        [
            sent,
            shape((TERMS * block, near + far), BF16),
            tile(F32),
            tile(F32),
            shape((areas * tiles * PAIR, depth * block), BF16),
            elder,
            *[tile(BF16)] * (depth - 2),
        ],
        [stay(v) for v in given],
        [pltpu.VMEM(v.shape, v.dtype) for v in given[:-1]]
        + [pltpu.SMEM(area_sizes.shape, area_sizes.dtype)]
        + [pltpu.VMEM((far + -far % block, block), F32), sending[0]]
        + [pltpu.SemaphoreType.DMA((len(given),)), sending[1]],
        in_specs=[HBM] * len(given),
    )
    older, past = rest[:1], rest[1:]
    swap = lambda v, bits: lax.ppermute(v, "nrn", [(i, i ^ bits) for i in range(group)])
    for iteration in range(STEPS):
        final = iteration == STEPS - 1
        mates = [swap(past[0], bits) for bits in range(1, group)]
        received = lax.all_to_all(
            outgoing.reshape(areas * group, PAIR, -1),
            ("area", "nrn"),
            split_axis=0,
            concat_axis=0,
            tiled=True,
        )
        received, mates = lax.optimization_barrier((received, mates))
        more = iteration < STEPS - 2
        picking = [] if final else [choice, *older, *past[1:]]
        result = call(
            functools.partial(step_kernel, group, len(picking)),
            [tile(F32)] if final else [sent, tile(F32), tile(BF16)] + [elder] * more,
            [weights, received, state, drive, rate, past[0], *mates]
            + picking,
            sending * (not final) + [pltpu.VMEM((near, stimuli), BF16)],
        )
        if final:
            return result[0]
        outgoing, state, newest, *older = result
        past = [newest, *past[:-1]]


def solution(mesh):
    placed = (
        P(None, ("area", "nrn"), None),
        P(("area", "nrn"), None),
        P(("area", "nrn")),
        P(("area", "nrn"), None),
        P(("area", "nrn"), None, None),
        P(("area", "nrn"), None, None),
        P("area", None),
        P("area"),
    )
    return jax.shard_map(
        functools.partial(local, mesh.shape["nrn"]),
        mesh=mesh,
        in_specs=placed,
        out_specs=P(("area", "nrn"), None),
        check_vma=False,
    )
```

```python
import functools
import math

import jax
import jax.numpy as jnp
from jax import lax
from jax.experimental import pallas as pl
from jax.experimental.pallas import tpu as pltpu
from jax.sharding import PartitionSpec as P

STEPS = 6
PAIR = 2
TERMS = 3
F32, BF16 = jnp.float32, jnp.bfloat16
VMEM = pl.BlockSpec(memory_space=pltpu.VMEM)
HBM = pl.BlockSpec(memory_space=pl.ANY)


def iota(shape, axis):
    return lax.broadcasted_iota(jnp.int32, shape, axis)


def terms_of(values):
    terms = []
    for _ in range(TERMS):
        terms.append(values.astype(BF16))
        values = values - terms[-1].astype(F32)
    return terms


def column(line):
    width = line.shape[1]
    eye = iota((width, width), 0) == iota((width, width), 1)
    return jnp.sum(jnp.where(eye, jnp.broadcast_to(line, eye.shape), 0.0), axis=1, keepdims=True)


def send(picked, chunks, out_ref, sems):
    stimuli = picked.shape[1]
    areas = chunks.shape[0]
    for tile in range(chunks.shape[2] // stimuli):
        for area in range(areas):
            start = (tile * areas + area) * PAIR
            chunks[area, :, tile * stimuli : (tile + 1) * stimuli] = picked[start : start + PAIR]
    copies = [
        pltpu.make_async_copy(chunks, out_ref.at[member], sems.at[member])
        for member in range(out_ref.shape[0])
    ]
    for copy in copies:
        copy.start()
    return copies


def rows_from(chunks, stimuli):
    tiles = [chunks[:, :, start : start + stimuli] for start in range(0, chunks.shape[2], stimuli)]
    return jnp.concatenate([tile.reshape(-1, stimuli) for tile in tiles], axis=0)


def pack_kernel(group, senders, *refs):
    given, outs, scratch = refs[:7], refs[7:-11], refs[-11:]
    held, (padded, chunks_ref, sems, send_sems) = scratch[:7], scratch[7:]
    outgoing, weights, state, rate, choice, older, *past = outs
    copies = [
        pltpu.make_async_copy(src, dst, sems.at[i]) for i, (src, dst) in enumerate(zip(given, held))
    ]
    for copy in copies:
        copy.start()
    for i in (4, 5, 6, 1, 0):
        copies[i].wait()
    history, leak, w_local, w_long, table, lags, sizes = held
    depth, block = history.shape[:2]
    areas = table.shape[0]
    me = lax.axis_index("nrn")
    active = (iota((block, 1), 0) + me * block < sizes[0]).astype(F32)
    state[...] = history[0] * active
    rate[...] = jnp.broadcast_to(active * column(leak[...]), rate.shape)

    tiles = -(-senders // PAIR)
    wide = (areas * PAIR, areas)
    mine = iota(wide, 1) == iota(wide, 0) // PAIR
    spread = jnp.dot(
        mine.astype(F32).astype(BF16), table[...].astype(F32).astype(BF16), preferred_element_type=F32
    )
    delay = jnp.broadcast_to(lags[...].astype(F32) - 1.0, wide)
    age = jnp.sum(jnp.where(mine, delay, 0.0), axis=1, keepdims=True)
    half = iota((areas * PAIR, 1), 0) % PAIR
    places = []
    for tile in range(tiles):
        sender = half * tiles + tile
        row = jnp.sum(jnp.where(iota(spread.shape, 1) == sender, spread, 0.0), axis=1, keepdims=True)
        places.append(row + jnp.where(sender < senders, age, float(depth)) * block)
    lanes = iota(choice.shape, 1).astype(F32)
    choice[...] = (lanes == jnp.concatenate(places, axis=0)).astype(F32).astype(BF16)
    rows = [(history[age] * active).astype(BF16) for age in range(depth)]
    picked = jnp.dot(choice[...], jnp.concatenate(rows, axis=0), preferred_element_type=F32)
    sent = send(picked.astype(BF16), chunks_ref, outgoing, send_sems)
    older[...] = jnp.dot(
        choice[:, block:], jnp.concatenate(rows[:-1], axis=0), preferred_element_type=F32
    )
    for ref, values in zip(past, rows):
        ref[...] = values

    for i in (2, 3):
        copies[i].wait()
    near = w_local.shape[1]
    for term, values in enumerate(terms_of(w_local[...])):
        weights[term * block : (term + 1) * block, :near] = values
    chunks = areas * group
    far = tiles * chunks * PAIR
    last = (tiles - 1) * chunks * PAIR
    padded[last:, :] = jnp.zeros((padded.shape[0] - last, block), F32)
    for area in range(areas):
        for member in range(group):
            for side in range(PAIR):
                first = side * tiles
                count = min(tiles, senders - first)
                rows = pl.ds((member * areas + area) * PAIR + side, count, stride=chunks * PAIR)
                padded[rows, :] = w_long[member, pl.ds(area * senders + first, count), :]
    for part in range(padded.shape[0] // block):
        tile = padded[part * block : (part + 1) * block, :].T
        width = min(block, far - part * block)
        for term, values in enumerate(terms_of(tile)):
            spot = near + part * block
            weights[term * block : (term + 1) * block, spot : spot + width] = values[:, :width]
    for copy in sent:
        copy.wait()


def step_kernel(group, left, *refs):
    (weights, received, state, drive, rate), mates = refs[:5], refs[5 : 5 + group]
    refs = refs[5 + group :]
    outs, current = refs[:-3] if left else refs[:-1], refs[-1]
    block = state.shape[0]
    near = group * block
    me = lax.axis_index("nrn")
    for slot in range(group):
        start = pl.multiple_of((me ^ slot) * block, block)
        current[pl.ds(start, block), :] = mates[slot][...]
    total = jnp.dot(weights[:, :near], current[...], preferred_element_type=F32)
    sent = rows_from(received[...], state.shape[1])
    total += jnp.dot(weights[:, near:], sent, preferred_element_type=F32)
    parts = [total[term * block : (term + 1) * block] for term in range(TERMS)]
    inputs = functools.reduce(lambda a, b: a + b, reversed(parts)) + drive[...]
    old = state[...]
    new = old + rate[...] * (jnp.tanh(inputs) - old)
    if not left:
        outs[0][...] = new
        return
    (choice, older, *past), (outgoing, new_state, newest, *next_older) = outs[:left], outs[left:]
    rounded = new.astype(BF16)
    picked = older[...] + jnp.dot(choice[:, :block], rounded, preferred_element_type=F32)
    copies = send(picked.astype(BF16), refs[-3], outgoing, refs[-2])
    new_state[...] = new
    newest[...] = rounded
    rows = jnp.concatenate([rounded, mates[0][...]] + [ref[...] for ref in past], axis=0)
    for ref in next_older:
        ref[...] = jnp.dot(choice[:, block:], rows, preferred_element_type=F32)
    for copy in copies:
        copy.wait()


def call(kernel, out_shape, operands, scratch=(), **settings):
    size = lambda value: math.prod(value.shape) * value.dtype.itemsize
    held = sum(map(size, [*out_shape, *operands]))
    return pl.pallas_call(
        kernel,
        out_shape=out_shape,
        out_specs=[HBM if len(value.shape) == 4 else VMEM for value in out_shape],
        compiler_params=pltpu.CompilerParams(vmem_limit_bytes=held + (4 << 20)),
        scratch_shapes=scratch,
        **{"in_specs": [VMEM] * len(operands), **settings},
    )(*operands)


def local(group, history, drive, leak, w_local, w_long, sender_rows, delays, area_sizes):
    depth, block, stimuli = history.shape
    areas, senders = sender_rows.shape[1:]
    tiles = -(-senders // PAIR)
    near, far = group * block, areas * group * tiles * PAIR
    shape = jax.ShapeDtypeStruct
    tile = lambda kind: shape((block, stimuli), kind)
    sent = shape((group, areas, PAIR, tiles * stimuli), BF16)
    elder = shape((areas * tiles * PAIR, stimuli), F32)
    sending = [pltpu.VMEM((areas, PAIR, tiles * stimuli), BF16), pltpu.SemaphoreType.DMA((group,))]
    given = [
        history,
        leak.reshape(1, block),
        w_local,
        w_long.transpose(1, 2, 0),
        sender_rows[0],
        delays,
        area_sizes,
    ]
    stay = lambda v: pltpu.with_memory_space_constraint(v, pltpu.HBM) if v.size > 1 else v
    outgoing, weights, state, rate, choice, *rest = call(
        functools.partial(pack_kernel, group, senders),
        [
            sent,
            shape((TERMS * block, near + far), BF16),
            tile(F32),
            tile(F32),
            shape((areas * tiles * PAIR, depth * block), BF16),
            elder,
            *[tile(BF16)] * (depth - 2),
        ],
        [stay(v) for v in given],
        [pltpu.VMEM(v.shape, v.dtype) for v in given[:-1]]
        + [pltpu.SMEM(area_sizes.shape, area_sizes.dtype)]
        + [pltpu.VMEM((far + -far % block, block), F32), sending[0]]
        + [pltpu.SemaphoreType.DMA((len(given),)), sending[1]],
        in_specs=[HBM] * len(given),
    )
    older, past = rest[:1], rest[1:]
    swap = lambda v, bits: lax.ppermute(v, "nrn", [(i, i ^ bits) for i in range(group)])
    for iteration in range(STEPS):
        final = iteration == STEPS - 1
        mates = [swap(past[0], bits) for bits in range(1, group)]
        received = lax.all_to_all(
            outgoing.reshape(group * areas, PAIR, -1),
            ("nrn", "area"),
            split_axis=0,
            concat_axis=0,
            tiled=True,
        )
        received, mates = lax.optimization_barrier((received, mates))
        more = iteration < STEPS - 2
        picking = [] if final else [choice, *older, *past[1:]]
        result = call(
            functools.partial(step_kernel, group, len(picking)),
            [tile(F32)] if final else [sent, tile(F32), tile(BF16)] + [elder] * more,
            [weights, received, state, drive, rate, past[0], *mates]
            + picking,
            sending * (not final) + [pltpu.VMEM((near, stimuli), BF16)],
        )
        if final:
            return result[0]
        outgoing, state, newest, *older = result
        past = [newest, *past[:-1]]


def solution(mesh):
    placed = (
        P(None, ("area", "nrn"), None),
        P(("area", "nrn"), None),
        P(("area", "nrn")),
        P(("area", "nrn"), None),
        P(("area", "nrn"), None, None),
        P(("area", "nrn"), None, None),
        P("area", None),
        P("area"),
    )
    return jax.shard_map(
        functools.partial(local, mesh.shape["nrn"]),
        mesh=mesh,
        in_specs=placed,
        out_specs=P(("area", "nrn"), None),
        check_vma=False,
    )
```

```python
import functools
import math

import jax
import jax.numpy as jnp
from jax import lax
from jax.experimental import pallas as pl
from jax.experimental.pallas import tpu as pltpu
from jax.sharding import PartitionSpec as P

STEPS = 6
PAIR = 2
TERMS = 3
F32, BF16 = jnp.float32, jnp.bfloat16
VMEM = pl.BlockSpec(memory_space=pltpu.VMEM)
HBM = pl.BlockSpec(memory_space=pl.ANY)


def iota(shape, axis):
    return lax.broadcasted_iota(jnp.int32, shape, axis)


def terms_of(values):
    terms = []
    for _ in range(TERMS):
        terms.append(values.astype(BF16))
        values = values - terms[-1].astype(F32)
    return terms


def column(line):
    width = line.shape[1]
    eye = iota((width, width), 0) == iota((width, width), 1)
    return jnp.sum(jnp.where(eye, jnp.broadcast_to(line, eye.shape), 0.0), axis=1, keepdims=True)


def send(picked, chunks, out_ref, sems):
    stimuli = picked.shape[1]
    areas = chunks.shape[0]
    for tile in range(chunks.shape[2] // stimuli):
        for area in range(areas):
            start = (tile * areas + area) * PAIR
            chunks[area, :, tile * stimuli : (tile + 1) * stimuli] = picked[start : start + PAIR]
    copies = [
        pltpu.make_async_copy(chunks, out_ref.at[member], sems.at[member])
        for member in range(out_ref.shape[0])
    ]
    for place, copy in enumerate(copies):
        copy.start(priority=place % 2)
    return copies


def rows_from(chunks, stimuli):
    tiles = [chunks[:, :, start : start + stimuli] for start in range(0, chunks.shape[2], stimuli)]
    return jnp.concatenate([tile.reshape(-1, stimuli) for tile in tiles], axis=0)


def pack_kernel(group, senders, *refs):
    given, outs, scratch = refs[:7], refs[7:-11], refs[-11:]
    held, (padded, chunks_ref, sems, send_sems) = scratch[:7], scratch[7:]
    outgoing, weights, state, rate, choice, older, *past = outs
    copies = [
        pltpu.make_async_copy(src, dst, sems.at[i]) for i, (src, dst) in enumerate(zip(given, held))
    ]
    for copy in copies:
        copy.start()
    for i in (4, 5, 6, 1, 0):
        copies[i].wait()
    history, leak, w_local, w_long, table, lags, sizes = held
    depth, block = history.shape[:2]
    areas = table.shape[0]
    me = lax.axis_index("nrn")
    active = (iota((block, 1), 0) + me * block < sizes[0]).astype(F32)
    state[...] = history[0] * active
    rate[...] = jnp.broadcast_to(active * column(leak[...]), rate.shape)

    tiles = -(-senders // PAIR)
    wide = (areas * PAIR, areas)
    mine = iota(wide, 1) == iota(wide, 0) // PAIR
    spread = jnp.dot(
        mine.astype(F32).astype(BF16), table[...].astype(F32).astype(BF16), preferred_element_type=F32
    )
    delay = jnp.broadcast_to(lags[...].astype(F32) - 1.0, wide)
    age = jnp.sum(jnp.where(mine, delay, 0.0), axis=1, keepdims=True)
    half = iota((areas * PAIR, 1), 0) % PAIR
    places = []
    for tile in range(tiles):
        sender = half * tiles + tile
        row = jnp.sum(jnp.where(iota(spread.shape, 1) == sender, spread, 0.0), axis=1, keepdims=True)
        places.append(row + jnp.where(sender < senders, age, float(depth)) * block)
    lanes = iota(choice.shape, 1).astype(F32)
    choice[...] = (lanes == jnp.concatenate(places, axis=0)).astype(F32).astype(BF16)
    rows = [(history[age] * active).astype(BF16) for age in range(depth)]
    picked = jnp.dot(choice[...], jnp.concatenate(rows, axis=0), preferred_element_type=F32)
    sent = send(picked.astype(BF16), chunks_ref, outgoing, send_sems)
    older[...] = jnp.dot(
        choice[:, block:], jnp.concatenate(rows[:-1], axis=0), preferred_element_type=F32
    )
    for ref, values in zip(past, rows):
        ref[...] = values

    for i in (2, 3):
        copies[i].wait()
    near = w_local.shape[1]
    for term, values in enumerate(terms_of(w_local[...])):
        weights[term * block : (term + 1) * block, :near] = values
    chunks = areas * group
    far = tiles * chunks * PAIR
    last = (tiles - 1) * chunks * PAIR
    padded[last:, :] = jnp.zeros((padded.shape[0] - last, block), F32)
    for area in range(areas):
        for member in range(group):
            for side in range(PAIR):
                first = side * tiles
                count = min(tiles, senders - first)
                rows = pl.ds((member * areas + area) * PAIR + side, count, stride=chunks * PAIR)
                padded[rows, :] = w_long[member, pl.ds(area * senders + first, count), :]
    for part in range(padded.shape[0] // block):
        tile = padded[part * block : (part + 1) * block, :].T
        width = min(block, far - part * block)
        for term, values in enumerate(terms_of(tile)):
            spot = near + part * block
            weights[term * block : (term + 1) * block, spot : spot + width] = values[:, :width]
    for copy in sent:
        copy.wait()


def step_kernel(group, left, *refs):
    (weights, received, state, drive, rate), mates = refs[:5], refs[5 : 5 + group]
    refs = refs[5 + group :]
    outs, current = refs[:-3] if left else refs[:-1], refs[-1]
    block = state.shape[0]
    near = group * block
    me = lax.axis_index("nrn")
    for slot in range(group):
        start = pl.multiple_of((me ^ slot) * block, block)
        current[pl.ds(start, block), :] = mates[slot][...]
    total = jnp.dot(weights[:, :near], current[...], preferred_element_type=F32)
    sent = rows_from(received[...], state.shape[1])
    total += jnp.dot(weights[:, near:], sent, preferred_element_type=F32)
    parts = [total[term * block : (term + 1) * block] for term in range(TERMS)]
    inputs = functools.reduce(lambda a, b: a + b, reversed(parts)) + drive[...]
    old = state[...]
    new = old + rate[...] * (jnp.tanh(inputs) - old)
    if not left:
        outs[0][...] = new
        return
    (choice, older, *past), (outgoing, new_state, newest, *next_older) = outs[:left], outs[left:]
    rounded = new.astype(BF16)
    picked = older[...] + jnp.dot(choice[:, :block], rounded, preferred_element_type=F32)
    copies = send(picked.astype(BF16), refs[-3], outgoing, refs[-2])
    new_state[...] = new
    newest[...] = rounded
    rows = jnp.concatenate([rounded, mates[0][...]] + [ref[...] for ref in past], axis=0)
    for ref in next_older:
        ref[...] = jnp.dot(choice[:, block:], rows, preferred_element_type=F32)
    for copy in copies:
        copy.wait()


def call(kernel, out_shape, operands, scratch=(), **settings):
    size = lambda value: math.prod(value.shape) * value.dtype.itemsize
    held = sum(map(size, [*out_shape, *operands]))
    return pl.pallas_call(
        kernel,
        out_shape=out_shape,
        out_specs=[HBM if len(value.shape) == 4 else VMEM for value in out_shape],
        compiler_params=pltpu.CompilerParams(vmem_limit_bytes=held + (4 << 20)),
        scratch_shapes=scratch,
        **{"in_specs": [VMEM] * len(operands), **settings},
    )(*operands)


def local(group, history, drive, leak, w_local, w_long, sender_rows, delays, area_sizes):
    depth, block, stimuli = history.shape
    areas, senders = sender_rows.shape[1:]
    tiles = -(-senders // PAIR)
    near, far = group * block, areas * group * tiles * PAIR
    shape = jax.ShapeDtypeStruct
    tile = lambda kind: shape((block, stimuli), kind)
    sent = shape((group, areas, PAIR, tiles * stimuli), BF16)
    elder = shape((areas * tiles * PAIR, stimuli), F32)
    sending = [pltpu.VMEM((areas, PAIR, tiles * stimuli), BF16), pltpu.SemaphoreType.DMA((group,))]
    given = [
        history,
        leak.reshape(1, block),
        w_local,
        w_long.transpose(1, 2, 0),
        sender_rows[0],
        delays,
        area_sizes,
    ]
    stay = lambda v: pltpu.with_memory_space_constraint(v, pltpu.HBM) if v.size > 1 else v
    outgoing, weights, state, rate, choice, *rest = call(
        functools.partial(pack_kernel, group, senders),
        [
            sent,
            shape((TERMS * block, near + far), BF16),
            tile(F32),
            tile(F32),
            shape((areas * tiles * PAIR, depth * block), BF16),
            elder,
            *[tile(BF16)] * (depth - 2),
        ],
        [stay(v) for v in given],
        [pltpu.VMEM(v.shape, v.dtype) for v in given[:-1]]
        + [pltpu.SMEM(area_sizes.shape, area_sizes.dtype)]
        + [pltpu.VMEM((far + -far % block, block), F32), sending[0]]
        + [pltpu.SemaphoreType.DMA((len(given),)), sending[1]],
        in_specs=[HBM] * len(given),
    )
    older, past = rest[:1], rest[1:]
    swap = lambda v, bits: lax.ppermute(v, "nrn", [(i, i ^ bits) for i in range(group)])
    for iteration in range(STEPS):
        final = iteration == STEPS - 1
        mates = [swap(past[0], bits) for bits in range(1, group)]
        received = lax.all_to_all(
            outgoing.reshape(group * areas, PAIR, -1),
            ("nrn", "area"),
            split_axis=0,
            concat_axis=0,
            tiled=True,
        )
        received, mates = lax.optimization_barrier((received, mates))
        more = iteration < STEPS - 2
        picking = [] if final else [choice, *older, *past[1:]]
        result = call(
            functools.partial(step_kernel, group, len(picking)),
            [tile(F32)] if final else [sent, tile(F32), tile(BF16)] + [elder] * more,
            [weights, received, state, drive, rate, past[0], *mates]
            + picking,
            sending * (not final) + [pltpu.VMEM((near, stimuli), BF16)],
        )
        if final:
            return result[0]
        outgoing, state, newest, *older = result
        past = [newest, *past[:-1]]


def solution(mesh):
    placed = (
        P(None, ("area", "nrn"), None),
        P(("area", "nrn"), None),
        P(("area", "nrn")),
        P(("area", "nrn"), None),
        P(("area", "nrn"), None, None),
        P(("area", "nrn"), None, None),
        P("area", None),
        P("area"),
    )
    return jax.shard_map(
        functools.partial(local, mesh.shape["nrn"]),
        mesh=mesh,
        in_specs=placed,
        out_specs=P(("area", "nrn"), None),
        check_vma=False,
    )
```

```python
import functools
import math

import jax
import jax.numpy as jnp
from jax import lax
from jax.experimental import pallas as pl
from jax.experimental.pallas import tpu as pltpu
from jax.sharding import PartitionSpec as P

STEPS = 6
PAIR = 2
TERMS = 3
F32, BF16 = jnp.float32, jnp.bfloat16
VMEM = pl.BlockSpec(memory_space=pltpu.VMEM)
HBM = pl.BlockSpec(memory_space=pl.ANY)


def iota(shape, axis):
    return lax.broadcasted_iota(jnp.int32, shape, axis)


def terms_of(values):
    terms = []
    for _ in range(TERMS):
        terms.append(values.astype(BF16))
        values = values - terms[-1].astype(F32)
    return terms


def column(line):
    width = line.shape[1]
    eye = iota((width, width), 0) == iota((width, width), 1)
    return jnp.sum(jnp.where(eye, jnp.broadcast_to(line, eye.shape), 0.0), axis=1, keepdims=True)


def send(picked, chunks, out_ref, sems):
    stimuli = picked.shape[1]
    areas = chunks.shape[0]
    for tile in range(chunks.shape[2] // stimuli):
        for area in range(areas):
            start = (tile * areas + area) * PAIR
            chunks[area, :, tile * stimuli : (tile + 1) * stimuli] = picked[start : start + PAIR]
    copies = [
        pltpu.make_async_copy(chunks, out_ref.at[member], sems.at[member])
        for member in range(out_ref.shape[0])
    ]
    for copy in copies:
        copy.start()
    return copies


def rows_from(chunks, stimuli):
    tiles = [chunks[:, :, start : start + stimuli] for start in range(0, chunks.shape[2], stimuli)]
    return jnp.concatenate([tile.reshape(-1, stimuli) for tile in tiles], axis=0)


def pack_kernel(group, senders, *refs):
    given, outs, scratch = refs[:7], refs[7:-11], refs[-11:]
    held, (padded, chunks_ref, sems, send_sems) = scratch[:7], scratch[7:]
    outgoing, weights, state, rate, choice, older, *past = outs
    copies = [
        pltpu.make_async_copy(src, dst, sems.at[i]) for i, (src, dst) in enumerate(zip(given, held))
    ]
    for copy in copies:
        copy.start()
    for i in (4, 5, 6, 1, 0):
        copies[i].wait()
    history, leak, w_local, w_long, table, lags, sizes = held
    depth, block = history.shape[:2]
    areas = table.shape[0]
    me = lax.axis_index("nrn")
    active = (iota((block, 1), 0) + me * block < sizes[0]).astype(F32)
    state[...] = history[0] * active
    rate[...] = jnp.broadcast_to(active * column(leak[...]), rate.shape)

    tiles = -(-senders // PAIR)
    wide = (areas * PAIR, areas)
    mine = iota(wide, 1) == iota(wide, 0) // PAIR
    spread = jnp.dot(
        mine.astype(F32).astype(BF16), table[...].astype(F32).astype(BF16), preferred_element_type=F32
    )
    delay = jnp.broadcast_to(lags[...].astype(F32) - 1.0, wide)
    age = jnp.sum(jnp.where(mine, delay, 0.0), axis=1, keepdims=True)
    half = iota((areas * PAIR, 1), 0) % PAIR
    places = []
    for tile in range(tiles):
        sender = half * tiles + tile
        row = jnp.sum(jnp.where(iota(spread.shape, 1) == sender, spread, 0.0), axis=1, keepdims=True)
        places.append(row + jnp.where(sender < senders, age, float(depth)) * block)
    lanes = iota(choice.shape, 1).astype(F32)
    choice[...] = (lanes == jnp.concatenate(places, axis=0)).astype(F32).astype(BF16)
    rows = [(history[age] * active).astype(BF16) for age in range(depth)]
    picked = jnp.dot(choice[...], jnp.concatenate(rows, axis=0), preferred_element_type=F32)
    sent = send(picked.astype(BF16), chunks_ref, outgoing, send_sems)
    older[...] = jnp.dot(
        choice[:, block:], jnp.concatenate(rows[:-1], axis=0), preferred_element_type=F32
    )
    for ref, values in zip(past, rows):
        ref[...] = values

    for i in (2, 3):
        copies[i].wait()
    near = w_local.shape[1]
    for term, values in enumerate(terms_of(w_local[...])):
        weights[term * block : (term + 1) * block, :near] = values
    chunks = areas * group
    far = tiles * chunks * PAIR
    last = (tiles - 1) * chunks * PAIR
    padded[last:, :] = jnp.zeros((padded.shape[0] - last, block), F32)
    for area in range(areas):
        for member in range(group):
            for side in range(PAIR):
                first = side * tiles
                count = min(tiles, senders - first)
                rows = pl.ds((member * areas + area) * PAIR + side, count, stride=chunks * PAIR)
                padded[rows, :] = w_long[member, pl.ds(area * senders + first, count), :]
    for part in range(padded.shape[0] // block):
        tile = padded[part * block : (part + 1) * block, :].T
        width = min(block, far - part * block)
        for term, values in enumerate(terms_of(tile)):
            spot = near + part * block
            weights[term * block : (term + 1) * block, spot : spot + width] = values[:, :width]
    for copy in sent:
        copy.wait()


def step_kernel(group, left, *refs):
    (weights, received, state, drive, rate), mates = refs[:5], refs[5 : 5 + group]
    refs = refs[5 + group :]
    outs, current = refs[:-3] if left else refs[:-1], refs[-1]
    block = state.shape[0]
    near = group * block
    me = lax.axis_index("nrn")
    for slot in range(group):
        start = pl.multiple_of((me ^ slot) * block, block)
        current[pl.ds(start, block), :] = mates[slot][...]
    current[near:, :] = rows_from(received[...], state.shape[1])
    total = jnp.dot(weights[...], current[...], preferred_element_type=F32)
    parts = [total[term * block : (term + 1) * block] for term in range(TERMS)]
    inputs = functools.reduce(lambda a, b: a + b, reversed(parts)) + drive[...]
    old = state[...]
    new = old + rate[...] * (jnp.tanh(inputs) - old)
    if not left:
        outs[0][...] = new
        return
    (choice, older, *past), (outgoing, new_state, newest, *next_older) = outs[:left], outs[left:]
    rounded = new.astype(BF16)
    picked = older[...] + jnp.dot(choice[:, :block], rounded, preferred_element_type=F32)
    copies = send(picked.astype(BF16), refs[-3], outgoing, refs[-2])
    new_state[...] = new
    newest[...] = rounded
    rows = jnp.concatenate([rounded, mates[0][...]] + [ref[...] for ref in past], axis=0)
    for ref in next_older:
        ref[...] = jnp.dot(choice[:, block:], rows, preferred_element_type=F32)
    for copy in copies:
        copy.wait()


def call(kernel, out_shape, operands, scratch=(), **settings):
    size = lambda value: math.prod(value.shape) * value.dtype.itemsize
    held = sum(map(size, [*out_shape, *operands]))
    return pl.pallas_call(
        kernel,
        out_shape=out_shape,
        out_specs=[HBM if len(value.shape) == 4 else VMEM for value in out_shape],
        compiler_params=pltpu.CompilerParams(vmem_limit_bytes=held + (4 << 20)),
        scratch_shapes=scratch,
        **{"in_specs": [VMEM] * len(operands), **settings},
    )(*operands)


def local(group, history, drive, leak, w_local, w_long, sender_rows, delays, area_sizes):
    depth, block, stimuli = history.shape
    areas, senders = sender_rows.shape[1:]
    tiles = -(-senders // PAIR)
    near, far = group * block, areas * group * tiles * PAIR
    shape = jax.ShapeDtypeStruct
    tile = lambda kind: shape((block, stimuli), kind)
    sent = shape((group, areas, PAIR, tiles * stimuli), BF16)
    elder = shape((areas * tiles * PAIR, stimuli), F32)
    sending = [pltpu.VMEM((areas, PAIR, tiles * stimuli), BF16), pltpu.SemaphoreType.DMA((group,))]
    given = [
        history,
        leak.reshape(1, block),
        w_local,
        w_long.transpose(1, 2, 0),
        sender_rows[0],
        delays,
        area_sizes,
    ]
    stay = lambda v: pltpu.with_memory_space_constraint(v, pltpu.HBM) if v.size > 1 else v
    outgoing, weights, state, rate, choice, *rest = call(
        functools.partial(pack_kernel, group, senders),
        [
            sent,
            shape((TERMS * block, near + far), BF16),
            tile(F32),
            tile(F32),
            shape((areas * tiles * PAIR, depth * block), BF16),
            elder,
            *[tile(BF16)] * (depth - 2),
        ],
        [stay(v) for v in given],
        [pltpu.VMEM(v.shape, v.dtype) for v in given[:-1]]
        + [pltpu.SMEM(area_sizes.shape, area_sizes.dtype)]
        + [pltpu.VMEM((far + -far % block, block), F32), sending[0]]
        + [pltpu.SemaphoreType.DMA((len(given),)), sending[1]],
        in_specs=[HBM] * len(given),
    )
    older, past = rest[:1], rest[1:]
    swap = lambda v, bits: lax.ppermute(v, "nrn", [(i, i ^ bits) for i in range(group)])
    for iteration in range(STEPS):
        final = iteration == STEPS - 1
        mates = [swap(past[0], bits) for bits in range(1, group)]
        received = lax.all_to_all(
            outgoing.reshape(group * areas, PAIR, -1),
            ("nrn", "area"),
            split_axis=0,
            concat_axis=0,
            tiled=True,
        )
        received, mates = lax.optimization_barrier((received, mates))
        more = iteration < STEPS - 2
        picking = [] if final else [choice, *older, *past[1:]]
        result = call(
            functools.partial(step_kernel, group, len(picking)),
            [tile(F32)] if final else [sent, tile(F32), tile(BF16)] + [elder] * more,
            [weights, received, state, drive, rate, past[0], *mates]
            + picking,
            sending * (not final) + [pltpu.VMEM((near + far, stimuli), BF16)],
        )
        if final:
            return result[0]
        outgoing, state, newest, *older = result
        past = [newest, *past[:-1]]


def solution(mesh):
    placed = (
        P(None, ("area", "nrn"), None),
        P(("area", "nrn"), None),
        P(("area", "nrn")),
        P(("area", "nrn"), None),
        P(("area", "nrn"), None, None),
        P(("area", "nrn"), None, None),
        P("area", None),
        P("area"),
    )
    return jax.shard_map(
        functools.partial(local, mesh.shape["nrn"]),
        mesh=mesh,
        in_specs=placed,
        out_specs=P(("area", "nrn"), None),
        check_vma=False,
    )
```
